32 devices in a mesh: col: 4 (over y, core), fac: 8 (over z, x).
Axes of the slice: x: 2, y: 2, z: 4, core: 2. Of those that a mesh axis runs over, the one named last changes fastest.
Arguments:
- facets: bfloat16 [2, 4096, 4096], P(None, 'col', 'fac'), may hold values from -6 to 6
- row_taper: float32 [4096], P('col'), may hold values from 0.5 to 1.5
- column_taper: float32 [4096], replicated, may hold values from 0.5 to 1.5
- column_place: int32 [1], replicated, may hold values from 0 to 511
- row_offset: int32 [4], replicated, may hold values from 0 to 4095
- column_offset: int32 [8], replicated, may hold values from 0 to 4095
- slot_subgrid: int32 [4, 8], replicated, may hold values from 0 to 7, each once within a row
Outputs:
- subgrids: float32 [4, 8, 2, 512, 128], P('col', 'fac')
The draws below stay inside these ranges and needn't reach their ends.
All inputs are finite; a program needn't handle non-finite values.
Results may differ from the reference program's by a relative error of at most 0.0052.
Values may be sent and summed in bfloat16 or wider, within the bound.
A program may use at most 64 MiB of HBM per device.

```python
import math
import jax
import jax.numpy as jnp
from jax import lax

FACET = 4096
STRIP = 128
SUBGRID = 512
FACET_COLS = 1
IMG_COLS = 4096
N_COL = 4
N_FAC = 8


def touch_ends(drawn, key, low, high):
    longest = drawn.shape.index(max(drawn.shape))
    spots = []
    for shift in (0, 1):
        where = [jax.random.randint(jax.random.fold_in(key, axis), (), 0, length) for axis, length in enumerate(drawn.shape)]
        where[longest] = (where[longest] + shift) % drawn.shape[longest]
        spots.append(tuple(where))
    return drawn.at[spots[0]].set(low).at[spots[1]].set(high)


def level_of(own_key, dims, cuts, least, high):
    factor_of, own = 1.0, jax.random.fold_in(own_key, 6)
    for position, blocks in cuts:
        heights = jnp.exp(jax.random.uniform(jax.random.fold_in(own, position), (blocks,), jnp.float32, least / len(cuts), high / len(cuts)))
        factor_of = factor_of * jnp.repeat(heights, dims[position] // blocks).reshape([-1 if axis == position else 1 for axis in range(len(dims))])
    return factor_of


def centred(key, extent, scale, bound, split=(), held_as=jnp.bfloat16):
    gain = level_of(key, extent, split, -0.22, 0.18) if split else 1.0
    result = jax.random.normal(key, extent, jnp.float32) * scale * gain
    return jnp.minimum(jnp.maximum(result, -bound), bound).astype(held_as)


def setup_inputs(seed: int = 0) -> dict:
    keys = jax.random.split(jax.random.key(seed), 8)
    facets = centred(keys[0], (2, FACET, IMG_COLS), 1.0, 6.0, ((1, 4), (2, 8)))
    row_taper = jnp.clip(0.5 + 1.0 * jax.random.uniform(keys[1], (FACET,), jnp.float32) ** level_of(keys[1], (FACET,), ((0, 4),), -0.2, 0.2), 0.5, 1.5)
    column_taper = jnp.clip(jax.random.uniform(keys[2], (FACET,), jnp.float32, 0.5, 1.5), 0.5, 1.5)
    column_place = jax.random.randint(keys[3], (FACET_COLS,), 0, SUBGRID).astype(jnp.int32)
    row_offset = touch_ends(jax.random.randint(keys[4], (N_COL,), 0, FACET), jax.random.fold_in(keys[4], 1), 0, FACET - 1).astype(jnp.int32)
    column_offset = touch_ends(jax.random.randint(keys[5], (N_FAC,), 0, FACET), jax.random.fold_in(keys[5], 1), 0, FACET - 1).astype(jnp.int32)
    slot_subgrid = jax.vmap(lambda own: jax.random.permutation(own, N_FAC))(jax.random.split(keys[6], N_COL)).reshape((N_COL, N_FAC)).astype(jnp.int32)
    return {"facets": facets, "row_taper": row_taper, "column_taper": column_taper, "column_place": column_place, "row_offset": row_offset, "column_offset": column_offset, "slot_subgrid": slot_subgrid}


def phase_table(starts, positions):
    offsets = jnp.arange(STRIP, dtype=jnp.int32)
    frequency = (starts[:, None] + offsets[None, :]) % FACET
    phases = frequency[:, :, None] * positions[None, None, :] % FACET
    angles = phases.astype(jnp.float32) * (2.0 * math.pi / FACET)
    norm_scale = 1.0 / math.sqrt(FACET)
    return jnp.stack([jnp.cos(angles) * norm_scale, -jnp.sin(angles) * norm_scale]).astype(jnp.bfloat16)

def complex_rows(table_rows, real_part, imag_part):
    row_total = table_rows.shape[1]
    stacked = table_rows.reshape(2 * row_total, table_rows.shape[2])
    first_product = jnp.dot(stacked, real_part, preferred_element_type=jnp.float32)
    second = jnp.dot(stacked, imag_part, preferred_element_type=jnp.float32)
    return (first_product[:row_total] - second[row_total:], second[:row_total] + first_product[row_total:])

def complex_cols(table_rows, real_part, imag_part):
    row_total = table_rows.shape[1]
    stacked = table_rows.reshape(2 * row_total, table_rows.shape[2])
    contract_dims = (((1,), (1,)), ((), ()))
    first_product = lax.dot_general(stacked, real_part, contract_dims, preferred_element_type=jnp.float32)
    second = lax.dot_general(stacked, imag_part, contract_dims, preferred_element_type=jnp.float32)
    return (first_product[:row_total] - second[row_total:], second[:row_total] + first_product[row_total:])

def reference(facets, row_taper, column_taper, column_place, row_offset, column_offset, slot_subgrid):
    column_gain = jnp.tile(column_taper, FACET_COLS)
    prepared = (facets.astype(jnp.float32) * row_taper[None, :, None] * column_gain[None, None, :]).astype(jnp.bfloat16)
    positions = jnp.arange(FACET, dtype=jnp.int32)
    offsets = jnp.arange(STRIP, dtype=jnp.int32)
    column_targets = (column_place[:, None] + offsets[None, :]) % SUBGRID

    def one_group(column_group):
        encode = phase_table(row_offset[column_group][None], positions)[:, 0]
        real_out, imag_out = complex_rows(encode, prepared[0], prepared[1])
        strip = lax.optimization_barrier(jnp.stack([real_out, imag_out]).astype(jnp.bfloat16))
        starts = column_offset[slot_subgrid[column_group]]
        decode = phase_table(starts, positions).reshape(2, N_FAC * STRIP, FACET)

        def add_facet(summed, facet_col):
            part_real = lax.dynamic_slice_in_dim(strip[0], facet_col * FACET, FACET, 1)
            part_imag = lax.dynamic_slice_in_dim(strip[1], facet_col * FACET, FACET, 1)
            real_part, imag_part = complex_cols(decode, part_real, part_imag)
            contribution = jnp.stack([real_part.reshape(N_FAC, STRIP, STRIP), imag_part.reshape(N_FAC, STRIP, STRIP)], axis=1)
            summed = summed.at[:, :, column_targets[facet_col], :].add(contribution)
            return (summed, None)
        summed, unused = lax.scan(add_facet, jnp.zeros((N_FAC, 2, SUBGRID, STRIP), jnp.float32), jnp.arange(FACET_COLS, dtype=jnp.int32))
        return summed
    return lax.map(one_group, jnp.arange(N_COL, dtype=jnp.int32))
```

```python
import functools
import math

import jax
import jax.numpy as jnp
from jax import lax
from jax.experimental import pallas as pl
from jax.experimental.pallas import tpu as pltpu
from jax.sharding import PartitionSpec as P

FACET = 4096
STRIP = 128
SUBGRID = 512
FINE = 16
CHUNKS = 4
CHUNK = STRIP // CHUNKS
MESH = pl.DeviceIdType.MESH


def unit_phase(phases):
    quarter = FACET // 4
    shifted = phases + quarter // 2
    angle = ((shifted & (quarter - 1)) - quarter // 2).astype(jnp.float32) * (2.0 * math.pi / FACET)
    turn = lax.shift_right_logical(shifted & (FACET - 1), quarter.bit_length() - 1)
    sq = angle * angle
    cosine = 1.0 + sq * (-1 / 2 + sq * (1 / 24 + sq * (-1 / 720 + sq * (1 / 40320))))
    sine = angle * (1.0 + sq * (-1 / 6 + sq * (1 / 120 + sq * (-1 / 5040 + sq * (1 / 362880)))))
    odd = (turn & 1) == 1
    first = jnp.where(odd, sine, cosine)
    second = jnp.where(odd, cosine, sine)
    real = jnp.where(((turn + 1) & 2) == 2, -first, first)
    imag = jnp.where((turn & 2) == 2, second, -second)
    return real, imag


def iota(shape, dim):
    return lax.broadcasted_iota(jnp.int32, shape, dim)


def kernel(
    cols, facs,
    row_offset, column_offset, slot_subgrid, column_place, row_taper, column_taper, facets,
    out,
    held, coarse_r, coarse_i, fine_r, fine_i, encode, decode_r, decode_i,
    pair_out, pair_in, far_part, far_out, far_in, own_part, strip, strip_in,
    half, mine, slots_out, slots_in,
    held_sem, pair_send, pair_recv, far_send, far_recv, strip_send, strip_recv, slot_send, slot_recv,
):
    col = lax.axis_index("col")
    fac = lax.axis_index("fac")
    col_hi, core = col // 2, col % 2
    fac_hi, fac_lo = fac // 2, fac % 2
    highs, zs = cols // 2, facs // 2
    rows, width = facets.shape[1], facets.shape[2]

    pair_id = (col_hi * 2 + 1 - core, fac)
    far_ids = [((col_hi + d) % highs * 2 + core, fac) for d in range(1, highs)]
    strip_id = (col, fac_hi * 2 + 1 - fac_lo)
    slot_ids = [(col, (fac_hi + d) % zs * 2 + fac_lo) for d in range(1, zs)]
    peers = [pair_id, *far_ids, strip_id, *slot_ids]
    barrier = pltpu.get_barrier_semaphore()
    for peer in peers:
        pl.semaphore_signal(barrier, inc=1, device_id=peer, device_id_type=MESH)
    loads = [pltpu.make_async_copy(facets.at[p], held.at[p], held_sem.at[p]) for p in range(2)]
    for load in loads:
        load.start()

    steps = STRIP // FINE
    position = col * rows + iota((1, rows), 1)
    fine_r[...], fine_i[...] = unit_phase(iota((FINE, rows), 0) * position)
    gain = row_taper[...] * (1.0 / math.sqrt(FACET))

    def encode_group(index, group):
        first = (row_offset[group] + FINE * iota((steps, rows), 0)) & (FACET - 1)
        real, imag = unit_phase(first * position)
        coarse_r[...] = real * gain
        coarse_i[...] = imag * gain

        def row(i, carry):
            ar, ai = coarse_r[pl.ds(i, 1), :], coarse_i[pl.ds(i, 1), :]
            br, bi = fine_r[...], fine_i[...]
            at = pl.multiple_of(i * FINE, FINE)
            encode[index, pl.ds(at, FINE), :] = (ar * br - ai * bi).astype(jnp.bfloat16)
            encode[index, pl.ds(at + STRIP, FINE), :] = (ar * bi + ai * br).astype(jnp.bfloat16)
            return carry

        lax.fori_loop(0, steps, row, 0)

    def product(index):
        table = encode[index]
        by_real = jnp.dot(table, held[0], preferred_element_type=jnp.float32)
        by_imag = jnp.dot(table, held[1], preferred_element_type=jnp.float32)
        return by_real[:STRIP] - by_imag[STRIP:], by_imag[:STRIP] + by_real[STRIP:]

    def chunked(target, real, imag):
        for j in range(CHUNKS):
            span = slice(j * CHUNK, (j + 1) * CHUNK)
            target[j, :CHUNK] = real[span].astype(target.dtype)
            target[j, CHUNK:] = imag[span].astype(target.dtype)

    def pair_copy(d, j):
        return pltpu.make_async_remote_copy(
            src_ref=pair_out.at[d, j], dst_ref=pair_in.at[d, j], send_sem=pair_send.at[d, j],
            recv_sem=pair_recv.at[d, j], device_id=pair_id, device_id_type=MESH)

    def far_copy(d, j):
        return pltpu.make_async_remote_copy(
            src_ref=far_out.at[d - 1, j], dst_ref=far_in.at[d - 1, j], send_sem=far_send.at[d - 1, j],
            recv_sem=far_recv.at[d - 1, j], device_id=far_ids[d - 1], device_id_type=MESH)

    def strip_copy(j):
        return pltpu.make_async_remote_copy(
            src_ref=strip.at[j], dst_ref=strip_in.at[j], send_sem=strip_send.at[j],
            recv_sem=strip_recv.at[j], device_id=strip_id, device_id_type=MESH)

    def slot_copy(d, j):
        return pltpu.make_async_remote_copy(
            src_ref=slots_out.at[d - 1, j], dst_ref=slots_in.at[d - 1, j], send_sem=slot_send.at[d - 1, j],
            recv_sem=slot_recv.at[d - 1, j], device_id=slot_ids[d - 1], device_id_type=MESH)

    order = [*range(1, highs), 0]
    for d in order:
        high = (col_hi + d) % highs * 2
        encode_group(2 * d, high + 1 - core)
        encode_group(2 * d + 1, high + core)

    for load in loads:
        load.wait()
    pl.semaphore_wait(barrier, len(peers))

    def to_pair(d):
        chunked(pair_out.at[d], *product(2 * d))
        for j in range(CHUNKS):
            pair_copy(d, j).start()

    for d in range(1, highs):
        to_pair(d)
        chunked(far_part.at[d - 1], *product(2 * d + 1))
    to_pair(0)
    for d in range(1, highs):
        for j in range(CHUNKS):
            pair_copy(d, j).wait_recv()
            far_out[d - 1, j] = (far_part[d - 1, j] + pair_in[d, j].astype(jnp.float32)).astype(jnp.bfloat16)
            far_copy(d, j).start()
    chunked(own_part, *product(1))

    lanes = zs * STRIP
    coarse_n = width // FINE
    starts = []
    for d in range(zs):
        start = column_offset[slot_subgrid[col, (fac_hi + d) % zs * 2 + fac_lo]]
        starts.append((start + iota((1, STRIP), 1)) & (FACET - 1))
    frequency = jnp.concatenate(starts, axis=1)
    fine_real, fine_imag = unit_phase(iota((FINE, lanes), 0) * frequency)
    fine_real, fine_imag = fine_real * (1.0 / math.sqrt(FACET)), fine_imag * (1.0 / math.sqrt(FACET))
    for part, block in enumerate((fac, fac_hi * 2 + 1 - fac_lo)):
        base = part * width

        def row(i, carry, base=base, block=block):
            ar, ai = unit_phase((block * width + i * FINE) * frequency)
            at = pl.multiple_of(base + i * FINE, FINE)
            decode_r[pl.ds(at, FINE), :] = (ar * fine_real - ai * fine_imag).astype(jnp.bfloat16)
            decode_i[pl.ds(at, FINE), :] = (ar * fine_imag + ai * fine_real).astype(jnp.bfloat16)
            return carry

        lax.fori_loop(0, coarse_n, row, 0)

    column_gain = column_taper[:, pl.ds(pl.multiple_of(fac * width, width), width)]

    def decoded(block, part):
        span = slice(part * width, (part + 1) * width)
        by_real = jnp.dot(block, decode_r[span], preferred_element_type=jnp.float32)
        by_imag = jnp.dot(block, decode_i[span], preferred_element_type=jnp.float32)
        return jnp.concatenate(
            [by_real[:CHUNK] - by_imag[CHUNK:], by_imag[:CHUNK] + by_real[CHUNK:]], axis=0)

    def finish(j):
        strip_copy(j).wait_recv()
        total = half[j] + decoded(strip_in[j], 1)
        mine[j] = total[:, :STRIP]
        for d in range(1, zs):
            slots_out[d - 1, j] = total[:, d * STRIP:(d + 1) * STRIP].astype(jnp.bfloat16)
            slot_copy(d, j).start()

    for j in range(CHUNKS):
        pair_copy(0, j).wait_recv()
        total = own_part[j] + pair_in[0, j].astype(jnp.float32)
        for d in range(1, highs):
            far_copy(d, j).wait_recv()
            total = total + far_in[d - 1, j].astype(jnp.float32)
        strip[j] = (total * column_gain).astype(jnp.bfloat16)
        strip_copy(j).start()
        half[j] = decoded(strip[j], 0)
        if j:
            finish(j - 1)
    finish(CHUNKS - 1)

    place = (iota((SUBGRID, STRIP), 0) - column_place[0]) & (SUBGRID - 1)
    chosen = (place == iota((SUBGRID, STRIP), 1)).astype(jnp.bfloat16)
    sums = []
    for j in range(CHUNKS):
        total = mine[j]
        for d in range(1, zs):
            slot_copy(d, j).wait_recv()
            total = total + slots_in[d - 1, j].astype(jnp.float32)
        sums.append(total)
    for part in range(2):
        value = jnp.concatenate([s[part * CHUNK:(part + 1) * CHUNK] for s in sums], axis=0)
        placed = None
        for step in range(3):
            rounded = value.astype(jnp.bfloat16)
            term = lax.dot_general(chosen, rounded, (((1,), (1,)), ((), ())), preferred_element_type=jnp.float32)
            placed = term if placed is None else placed + term
            value = value - rounded.astype(jnp.float32)
        out[part] = placed

    for j in range(CHUNKS):
        for d in range(highs):
            pair_copy(d, j).wait_send()
        for d in range(1, highs):
            far_copy(d, j).wait_send()
        strip_copy(j).wait_send()
        for d in range(1, zs):
            slot_copy(d, j).wait_send()


def solution(mesh):
    cols, facs = mesh.shape["col"], mesh.shape["fac"]
    highs, zs = cols // 2, facs // 2

    def on_device(facets, row_taper, column_taper, column_place, row_offset, column_offset, slot_subgrid):
        rows, width = facets.shape[1], facets.shape[2]
        bf16, f32 = jnp.bfloat16, jnp.float32
        lanes = zs * STRIP
        part = (CHUNKS, 2 * CHUNK, width)
        slot = (CHUNKS, 2 * CHUNK, STRIP)
        far = max(highs - 1, 1)
        sem = pltpu.SemaphoreType.DMA
        smem = pl.BlockSpec(memory_space=pltpu.SMEM)
        vmem = pl.BlockSpec(memory_space=pltpu.VMEM)
        grid = pl.pallas_call(
            functools.partial(kernel, cols, facs),
            out_shape=jax.ShapeDtypeStruct((2, SUBGRID, STRIP), f32),
            in_specs=[smem] * 4 + [vmem] * 2 + [pl.BlockSpec(memory_space=pl.ANY)],
            out_specs=vmem,
            scratch_shapes=[
                pltpu.VMEM((2, rows, width), bf16),
                pltpu.VMEM((STRIP // FINE, rows), f32), pltpu.VMEM((STRIP // FINE, rows), f32),
                pltpu.VMEM((FINE, rows), f32), pltpu.VMEM((FINE, rows), f32),
                pltpu.VMEM((cols, 2 * STRIP, rows), bf16),
                pltpu.VMEM((2 * width, lanes), bf16), pltpu.VMEM((2 * width, lanes), bf16),
                pltpu.VMEM((highs, *part), bf16), pltpu.VMEM((highs, *part), bf16),
                pltpu.VMEM((far, *part), f32),
                pltpu.VMEM((far, *part), bf16), pltpu.VMEM((far, *part), bf16),
                pltpu.VMEM(part, f32),
                pltpu.VMEM(part, bf16), pltpu.VMEM(part, bf16),
                pltpu.VMEM((CHUNKS, 2 * CHUNK, lanes), f32),
                pltpu.VMEM(slot, f32),
                pltpu.VMEM((zs - 1, *slot), bf16), pltpu.VMEM((zs - 1, *slot), bf16),
                sem((2,)),
                sem((highs, CHUNKS)), sem((highs, CHUNKS)),
                sem((far, CHUNKS)), sem((far, CHUNKS)),
                sem((CHUNKS,)), sem((CHUNKS,)),
                sem((zs - 1, CHUNKS)), sem((zs - 1, CHUNKS)),
            ],
            compiler_params=pltpu.CompilerParams(
                collective_id=0, has_side_effects=True, vmem_limit_bytes=48 * 1024 * 1024),
        )(row_offset, column_offset, slot_subgrid, column_place,
          row_taper.reshape(1, -1), column_taper.reshape(1, -1), facets)
        return grid.reshape(1, 1, 2, SUBGRID, STRIP)

    in_specs = (P(None, "col", "fac"), P("col"), P(), P(), P(), P(), P())
    out_specs = P("col", "fac", None, None, None)
    return jax.shard_map(on_device, mesh=mesh, in_specs=in_specs, out_specs=out_specs, check_vma=False)
```

```python
import functools
import math

import jax
import jax.numpy as jnp
from jax import lax
from jax.experimental import pallas as pl
from jax.experimental.pallas import tpu as pltpu
from jax.sharding import PartitionSpec as P

FACET = 4096
STRIP = 128
SUBGRID = 512
FINE = 16
CHUNKS = 4
LAG = 2
CHUNK = STRIP // CHUNKS
MESH = pl.DeviceIdType.MESH


def unit_phase(phases):
    quarter = FACET // 4
    shifted = phases + quarter // 2
    angle = ((shifted & (quarter - 1)) - quarter // 2).astype(jnp.float32) * (2.0 * math.pi / FACET)
    turn = lax.shift_right_logical(shifted & (FACET - 1), quarter.bit_length() - 1)
    sq = angle * angle
    cosine = 1.0 + sq * (-1 / 2 + sq * (1 / 24 + sq * (-1 / 720 + sq * (1 / 40320))))
    sine = angle * (1.0 + sq * (-1 / 6 + sq * (1 / 120 + sq * (-1 / 5040 + sq * (1 / 362880)))))
    odd = (turn & 1) == 1
    first = jnp.where(odd, sine, cosine)
    second = jnp.where(odd, cosine, sine)
    real = jnp.where(((turn + 1) & 2) == 2, -first, first)
    imag = jnp.where((turn & 2) == 2, second, -second)
    return real, imag


def iota(shape, dim):
    return lax.broadcasted_iota(jnp.int32, shape, dim)


def kernel(
    cols, facs,
    row_offset_in, column_offset_in, slot_subgrid_in, row_taper_in, column_taper_in, facets,
    out,
    row_offset, column_offset, slot_subgrid, row_taper, column_gain, held, coarse_r, coarse_i, fine_r, fine_i, steep_r, steep_i, encode, decode_r, decode_i,
    pair_out, pair_in, far_part, far_out, far_in, own_part, strip, strip_in,
    half, mine, slots_out, slots_in,
    zeros, placed, out_sem, small_sem, held_sem, pair_send, pair_recv, far_send, far_recv, strip_send, strip_recv, slot_send, slot_recv,
):
    col = lax.axis_index("col")
    fac = lax.axis_index("fac")
    col_hi, core = col // 2, col % 2
    fac_hi, fac_lo = fac // 2, fac % 2
    highs, zs = cols // 2, facs // 2
    rows, width = facets.shape[1], facets.shape[2]

    pair_id = (col_hi * 2 + 1 - core, fac)
    far_ids = [((col_hi + d) % highs * 2 + core, fac) for d in range(1, highs)]
    strip_id = (col, fac_hi * 2 + 1 - fac_lo)
    slot_ids = [(col, (fac_hi + d) % zs * 2 + fac_lo) for d in range(1, zs)]
    peers = [pair_id, *far_ids, strip_id, *slot_ids]
    own_columns = pl.ds(pl.multiple_of(fac * width, width), width)
    small = [
        pltpu.make_async_copy(source, target, small_sem.at[n])
        for n, (source, target) in enumerate((
            (row_offset_in, row_offset), (column_offset_in, column_offset), (slot_subgrid_in, slot_subgrid),
            (row_taper_in, row_taper),
            (column_taper_in.at[:, own_columns], column_gain)))]
    loads = [pltpu.make_async_copy(facets.at[p], held.at[p], held_sem.at[p]) for p in range(2)]
    for load in (*small, *loads):
        load.start()
    barrier = pltpu.get_barrier_semaphore()
    for peer in peers:
        pl.semaphore_signal(barrier, inc=1, device_id=peer, device_id_type=MESH)

    steps = STRIP // FINE
    position = col * rows + iota((1, rows), 1)
    fine_r[...], fine_i[...] = unit_phase(iota((FINE, rows), 0) * position)
    for load in small:
        load.wait()
    gain = row_taper[...] * (1.0 / math.sqrt(FACET))

    def encode_group(index, group):
        first = (row_offset[group] + FINE * iota((steps, rows), 0)) & (FACET - 1)
        real, imag = unit_phase(first * position)
        coarse_r[...] = real * gain
        coarse_i[...] = imag * gain

        def row(i, carry):
            ar, ai = coarse_r[pl.ds(i, 1), :], coarse_i[pl.ds(i, 1), :]
            br, bi = fine_r[...], fine_i[...]
            at = pl.multiple_of(i * FINE, FINE)
            encode[index, pl.ds(at, FINE), :] = (ar * br - ai * bi).astype(jnp.bfloat16)
            encode[index, pl.ds(at + STRIP, FINE), :] = (ar * bi + ai * br).astype(jnp.bfloat16)
            return carry

        lax.fori_loop(0, steps, row, 0)

    def product(index):
        table = encode[index]
        by_real = jnp.dot(table, held[0], preferred_element_type=jnp.float32)
        by_imag = jnp.dot(table, held[1], preferred_element_type=jnp.float32)
        return by_real[:STRIP] - by_imag[STRIP:], by_imag[:STRIP] + by_real[STRIP:]

    def chunked(target, real, imag):
        for j in range(CHUNKS):
            span = slice(j * CHUNK, (j + 1) * CHUNK)
            target[j, :CHUNK] = real[span].astype(target.dtype)
            target[j, CHUNK:] = imag[span].astype(target.dtype)

    def pair_copy(d, j):
        return pltpu.make_async_remote_copy(
            src_ref=pair_out.at[d, j], dst_ref=pair_in.at[d, j], send_sem=pair_send.at[d, j],
            recv_sem=pair_recv.at[d, j], device_id=pair_id, device_id_type=MESH)

    def far_copy(d, j):
        return pltpu.make_async_remote_copy(
            src_ref=far_out.at[d - 1, j], dst_ref=far_in.at[d - 1, j], send_sem=far_send.at[d - 1, j],
            recv_sem=far_recv.at[d - 1, j], device_id=far_ids[d - 1], device_id_type=MESH)

    def strip_copy(j):
        return pltpu.make_async_remote_copy(
            src_ref=strip.at[j], dst_ref=strip_in.at[j], send_sem=strip_send.at[j],
            recv_sem=strip_recv.at[j], device_id=strip_id, device_id_type=MESH)

    def slot_copy(d, j):
        return pltpu.make_async_remote_copy(
            src_ref=slots_out.at[d - 1, j], dst_ref=slots_in.at[d - 1, j], send_sem=slot_send.at[d - 1, j],
            recv_sem=slot_recv.at[d - 1, j], device_id=slot_ids[d - 1], device_id_type=MESH)

    zeros[...] = jnp.zeros_like(zeros)
    blanks = [
        pltpu.make_async_copy(
            zeros, out.at[:, pl.ds(n * SUBGRID + STRIP, SUBGRID - STRIP), :], out_sem.at[0, n]) for n in range(2)]

    def groups(d):
        high = (col_hi + d) % highs * 2
        encode_group(2 * d, high + 1 - core)
        encode_group(2 * d + 1, high + core)

    for d in range(1, highs):
        groups(d)
    for load in loads:
        load.wait()
    for d in range(1, highs):
        chunked(pair_out.at[d], *product(2 * d))
        chunked(far_part.at[d - 1], *product(2 * d + 1))
    pl.semaphore_wait(barrier, len(peers))
    for d in range(1, highs):
        for j in range(CHUNKS):
            pair_copy(d, j).start()
    groups(0)
    chunked(pair_out.at[0], *product(0))
    for j in range(CHUNKS):
        pair_copy(0, j).start()
    for d in range(1, highs):
        for j in range(CHUNKS):
            pair_copy(d, j).wait_recv()
            far_out[d - 1, j] = (far_part[d - 1, j] + pair_in[d, j].astype(jnp.float32)).astype(jnp.bfloat16)
            far_copy(d, j).start()
    for blank in blanks:
        blank.start()
    chunked(own_part, *product(1))

    lanes = zs * STRIP
    coarse_n = width // FINE
    starts = []
    for d in range(zs):
        start = column_offset[slot_subgrid[col, (fac_hi + d) % zs * 2 + fac_lo]]
        starts.append((start + iota((1, STRIP), 1)) & (FACET - 1))
    frequency = jnp.concatenate(starts, axis=1)
    fine_real, fine_imag = unit_phase(iota((FINE, lanes), 0) * frequency)
    fine_real, fine_imag = fine_real * (1.0 / math.sqrt(FACET)), fine_imag * (1.0 / math.sqrt(FACET))
    for part, block in enumerate((fac, fac_hi * 2 + 1 - fac_lo)):
        base = part * width
        steep_r[...], steep_i[...] = unit_phase((block * width + FINE * iota((coarse_n, lanes), 0)) * frequency)

        def row(i, carry, base=base):
            ar, ai = steep_r[pl.ds(i, 1), :], steep_i[pl.ds(i, 1), :]
            at = pl.multiple_of(base + i * FINE, FINE)
            decode_r[pl.ds(at, FINE), :] = (ar * fine_real - ai * fine_imag).astype(jnp.bfloat16)
            decode_i[pl.ds(at, FINE), :] = (ar * fine_imag + ai * fine_real).astype(jnp.bfloat16)
            return carry

        lax.fori_loop(0, coarse_n, row, 0)

    def decoded(block, part):
        span = slice(part * width, (part + 1) * width)
        by_real = jnp.dot(block, decode_r[span], preferred_element_type=jnp.float32)
        by_imag = jnp.dot(block, decode_i[span], preferred_element_type=jnp.float32)
        return jnp.concatenate(
            [by_real[:CHUNK] - by_imag[CHUNK:], by_imag[:CHUNK] + by_real[CHUNK:]], axis=0)

    def finish(j):
        strip_copy(j).wait_recv()
        total = half[j] + decoded(strip_in[j], 1)
        mine[j] = total[:, :STRIP]
        for d in range(1, zs):
            slots_out[d - 1, j] = total[:, d * STRIP:(d + 1) * STRIP].astype(jnp.bfloat16)
            slot_copy(d, j).start()

    for j in range(CHUNKS):
        pair_copy(0, j).wait_recv()
        total = own_part[j] + pair_in[0, j].astype(jnp.float32)
        for d in range(1, highs):
            far_copy(d, j).wait_recv()
            total = total + far_in[d - 1, j].astype(jnp.float32)
        strip[j] = (total * column_gain[...]).astype(jnp.bfloat16)
        strip_copy(j).start()
        half[j] = decoded(strip[j], 0)
        if j >= LAG:
            finish(j - LAG)
    for j in range(CHUNKS - LAG, CHUNKS):
        finish(j)

    sums = []
    for j in range(CHUNKS):
        total = mine[j]
        for d in range(1, zs):
            slot_copy(d, j).wait_recv()
            total = total + slots_in[d - 1, j].astype(jnp.float32)
        sums.append(total)
    for part in range(2):
        value = jnp.concatenate([s[part * CHUNK:(part + 1) * CHUNK] for s in sums], axis=0)
        placed[part] = value.T

    puts = [
        pltpu.make_async_copy(placed, out.at[:, pl.ds(n * SUBGRID, STRIP), :], out_sem.at[1, n]) for n in range(2)]
    for put in puts:
        put.start()
    for j in range(CHUNKS):
        for d in range(highs):
            pair_copy(d, j).wait_send()
        for d in range(1, highs):
            far_copy(d, j).wait_send()
        strip_copy(j).wait_send()
        for d in range(1, zs):
            slot_copy(d, j).wait_send()
    for put in (*blanks, *puts):
        put.wait()


def solution(mesh):
    cols, facs = mesh.shape["col"], mesh.shape["fac"]
    highs, zs = cols // 2, facs // 2

    def on_device(facets, row_taper, column_taper, column_place, row_offset, column_offset, slot_subgrid):
        rows, width = facets.shape[1], facets.shape[2]
        bf16, f32 = jnp.bfloat16, jnp.float32
        lanes = zs * STRIP
        part = (CHUNKS, 2 * CHUNK, width)
        slot = (CHUNKS, 2 * CHUNK, STRIP)
        far = max(highs - 1, 1)
        sem = pltpu.SemaphoreType.DMA
        grid = pl.pallas_call(
            functools.partial(kernel, cols, facs),
            out_shape=jax.ShapeDtypeStruct((2, 2 * SUBGRID, STRIP), f32),
            in_specs=[pl.BlockSpec(memory_space=pltpu.HBM)] * 6,
            out_specs=pl.BlockSpec(memory_space=pl.ANY),
            scratch_shapes=[
                pltpu.SMEM(row_offset.shape, jnp.int32), pltpu.SMEM(column_offset.shape, jnp.int32),
                pltpu.SMEM(slot_subgrid.shape, jnp.int32),
                pltpu.VMEM((1, rows), f32), pltpu.VMEM((1, width), f32),
                pltpu.VMEM((2, rows, width), bf16),
                pltpu.VMEM((STRIP // FINE, rows), f32), pltpu.VMEM((STRIP // FINE, rows), f32),
                pltpu.VMEM((FINE, rows), f32), pltpu.VMEM((FINE, rows), f32),
                pltpu.VMEM((width // FINE, lanes), f32), pltpu.VMEM((width // FINE, lanes), f32),
                pltpu.VMEM((cols, 2 * STRIP, rows), bf16),
                pltpu.VMEM((2 * width, lanes), bf16), pltpu.VMEM((2 * width, lanes), bf16),
                pltpu.VMEM((highs, *part), bf16), pltpu.VMEM((highs, *part), bf16),
                pltpu.VMEM((far, *part), f32),
                pltpu.VMEM((far, *part), bf16), pltpu.VMEM((far, *part), bf16),
                pltpu.VMEM(part, f32),
                pltpu.VMEM(part, bf16), pltpu.VMEM(part, bf16),
                pltpu.VMEM((CHUNKS, 2 * CHUNK, lanes), f32),
                pltpu.VMEM(slot, f32),
                pltpu.VMEM((zs - 1, *slot), bf16), pltpu.VMEM((zs - 1, *slot), bf16),
                pltpu.VMEM((2, SUBGRID - STRIP, STRIP), f32), pltpu.VMEM((2, STRIP, STRIP), f32), sem((2, 2)),
                sem((5,)), sem((2,)),
                sem((highs, CHUNKS)), sem((highs, CHUNKS)),
                sem((far, CHUNKS)), sem((far, CHUNKS)),
                sem((CHUNKS,)), sem((CHUNKS,)),
                sem((zs - 1, CHUNKS)), sem((zs - 1, CHUNKS)),
            ],
            compiler_params=pltpu.CompilerParams(
                collective_id=0, has_side_effects=True, vmem_limit_bytes=67_043_328),
        )(row_offset, column_offset, slot_subgrid,
          row_taper.reshape(1, -1), column_taper.reshape(1, -1), facets)
        grid = lax.dynamic_slice_in_dim(grid, SUBGRID - column_place[0], SUBGRID, axis=1)
        return grid.reshape(1, 1, 2, SUBGRID, STRIP)

    in_specs = (P(None, "col", "fac"), P("col"), P(), P(), P(), P(), P())
    out_specs = P("col", "fac", None, None, None)
    return jax.shard_map(on_device, mesh=mesh, in_specs=in_specs, out_specs=out_specs, check_vma=False)
```

```python
import functools
import math

import jax
import jax.numpy as jnp
from jax import lax
from jax.experimental import pallas as pl
from jax.experimental.pallas import tpu as pltpu
from jax.sharding import PartitionSpec as P

FACET = 4096
STRIP = 128
SUBGRID = 512
FINE = 16
CHUNKS = 4
LAG = 2
CHUNK = STRIP // CHUNKS
MESH = pl.DeviceIdType.MESH


def unit_phase(phases):
    quarter = FACET // 4
    shifted = phases + quarter // 2
    angle = ((shifted & (quarter - 1)) - quarter // 2).astype(jnp.float32) * (2.0 * math.pi / FACET)
    turn = lax.shift_right_logical(shifted & (FACET - 1), quarter.bit_length() - 1)
    sq = angle * angle
    cosine = 1.0 + sq * (-1 / 2 + sq * (1 / 24 + sq * (-1 / 720 + sq * (1 / 40320))))
    sine = angle * (1.0 + sq * (-1 / 6 + sq * (1 / 120 + sq * (-1 / 5040 + sq * (1 / 362880)))))
    odd = (turn & 1) == 1
    first = jnp.where(odd, sine, cosine)
    second = jnp.where(odd, cosine, sine)
    real = jnp.where(((turn + 1) & 2) == 2, -first, first)
    imag = jnp.where((turn & 2) == 2, second, -second)
    return real, imag


def iota(shape, dim):
    return lax.broadcasted_iota(jnp.int32, shape, dim)


def kernel(
    cols, facs,
    row_offset_in, column_offset_in, slot_subgrid_in, row_taper_in, column_taper_in, facets,
    out,
    row_offset, column_offset, slot_subgrid, row_taper, column_gain, held, coarse_r, coarse_i, fine_r, fine_i, steep_r, steep_i, encode, decode_r, decode_i,
    pair_out, pair_in, far_part, far_out, far_in, own_part, strip, strip_in,
    half, mine, slots_out, slots_in,
    small_sem, held_sem, pair_send, pair_recv, far_send, far_recv, strip_send, strip_recv, slot_send, slot_recv,
):
    col = lax.axis_index("col")
    fac = lax.axis_index("fac")
    col_hi, core = col // 2, col % 2
    fac_hi, fac_lo = fac // 2, fac % 2
    highs, zs = cols // 2, facs // 2
    rows, width = facets.shape[1], facets.shape[2]

    pair_id = (col_hi * 2 + 1 - core, fac)
    far_ids = [((col_hi + d) % highs * 2 + core, fac) for d in range(1, highs)]
    strip_id = (col, fac_hi * 2 + 1 - fac_lo)
    slot_ids = [(col, (fac_hi + d) % zs * 2 + fac_lo) for d in range(1, zs)]
    peers = [pair_id, *far_ids, strip_id, *slot_ids]
    own_columns = pl.ds(pl.multiple_of(fac * width, width), width)
    small = [
        pltpu.make_async_copy(source, target, small_sem.at[n])
        for n, (source, target) in enumerate((
            (row_offset_in, row_offset), (column_offset_in, column_offset), (slot_subgrid_in, slot_subgrid),
            (row_taper_in, row_taper),
            (column_taper_in.at[:, own_columns], column_gain)))]
    loads = [pltpu.make_async_copy(facets.at[p], held.at[p], held_sem.at[p]) for p in range(2)]
    for load in (*small, *loads):
        load.start()
    barrier = pltpu.get_barrier_semaphore()
    for peer in peers:
        pl.semaphore_signal(barrier, inc=1, device_id=peer, device_id_type=MESH)

    steps = STRIP // FINE
    position = col * rows + iota((1, rows), 1)
    fine_r[...], fine_i[...] = unit_phase(iota((FINE, rows), 0) * position)
    for load in small:
        load.wait()
    gain = row_taper[...] * (1.0 / math.sqrt(FACET))

    def encode_group(index, group):
        first = (row_offset[group] + FINE * iota((steps, rows), 0)) & (FACET - 1)
        real, imag = unit_phase(first * position)
        coarse_r[...] = real * gain
        coarse_i[...] = imag * gain

        def row(i, carry):
            ar, ai = coarse_r[pl.ds(i, 1), :], coarse_i[pl.ds(i, 1), :]
            br, bi = fine_r[...], fine_i[...]
            at = pl.multiple_of(i * FINE, FINE)
            encode[index, pl.ds(at, FINE), :] = (ar * br - ai * bi).astype(jnp.bfloat16)
            encode[index, pl.ds(at + STRIP, FINE), :] = (ar * bi + ai * br).astype(jnp.bfloat16)
            return carry

        lax.fori_loop(0, steps, row, 0)

    def product(index):
        table = encode[index]
        by_real = jnp.dot(table, held[0], preferred_element_type=jnp.float32)
        by_imag = jnp.dot(table, held[1], preferred_element_type=jnp.float32)
        return by_real[:STRIP] - by_imag[STRIP:], by_imag[:STRIP] + by_real[STRIP:]

    def chunked(target, real, imag):
        for j in range(CHUNKS):
            span = slice(j * CHUNK, (j + 1) * CHUNK)
            target[j, :CHUNK] = real[span].astype(target.dtype)
            target[j, CHUNK:] = imag[span].astype(target.dtype)

    def pair_copy(d, j):
        return pltpu.make_async_remote_copy(
            src_ref=pair_out.at[d, j], dst_ref=pair_in.at[d, j], send_sem=pair_send.at[d, j],
            recv_sem=pair_recv.at[d, j], device_id=pair_id, device_id_type=MESH)

    def far_copy(d, j):
        return pltpu.make_async_remote_copy(
            src_ref=far_out.at[d - 1, j], dst_ref=far_in.at[d - 1, j], send_sem=far_send.at[d - 1, j],
            recv_sem=far_recv.at[d - 1, j], device_id=far_ids[d - 1], device_id_type=MESH)

    def strip_copy(j):
        return pltpu.make_async_remote_copy(
            src_ref=strip.at[j], dst_ref=strip_in.at[j], send_sem=strip_send.at[j],
            recv_sem=strip_recv.at[j], device_id=strip_id, device_id_type=MESH)

    def slot_copy(d, j):
        return pltpu.make_async_remote_copy(
            src_ref=slots_out.at[d - 1, j], dst_ref=slots_in.at[d - 1, j], send_sem=slot_send.at[d - 1, j],
            recv_sem=slot_recv.at[d - 1, j], device_id=slot_ids[d - 1], device_id_type=MESH)

    def groups(d):
        high = (col_hi + d) % highs * 2
        encode_group(2 * d, high + 1 - core)
        encode_group(2 * d + 1, high + core)

    for d in range(1, highs):
        groups(d)
    for load in loads:
        load.wait()
    for d in range(1, highs):
        chunked(pair_out.at[d], *product(2 * d))
        chunked(far_part.at[d - 1], *product(2 * d + 1))
    pl.semaphore_wait(barrier, len(peers))
    for d in range(1, highs):
        for j in range(CHUNKS):
            pair_copy(d, j).start()
    groups(0)
    chunked(pair_out.at[0], *product(0))
    for j in range(CHUNKS):
        pair_copy(0, j).start()
    for d in range(1, highs):
        for j in range(CHUNKS):
            pair_copy(d, j).wait_recv()
            far_out[d - 1, j] = (far_part[d - 1, j] + pair_in[d, j].astype(jnp.float32)).astype(jnp.bfloat16)
            far_copy(d, j).start()
    chunked(own_part, *product(1))

    lanes = zs * STRIP
    coarse_n = width // FINE
    starts = []
    for d in range(zs):
        start = column_offset[slot_subgrid[col, (fac_hi + d) % zs * 2 + fac_lo]]
        starts.append((start + iota((1, STRIP), 1)) & (FACET - 1))
    frequency = jnp.concatenate(starts, axis=1)
    fine_real, fine_imag = unit_phase(iota((FINE, lanes), 0) * frequency)
    fine_real, fine_imag = fine_real * (1.0 / math.sqrt(FACET)), fine_imag * (1.0 / math.sqrt(FACET))
    for part, block in enumerate((fac, fac_hi * 2 + 1 - fac_lo)):
        base = part * width
        steep_r[...], steep_i[...] = unit_phase((block * width + FINE * iota((coarse_n, lanes), 0)) * frequency)

        def row(i, carry, base=base):
            ar, ai = steep_r[pl.ds(i, 1), :], steep_i[pl.ds(i, 1), :]
            at = pl.multiple_of(base + i * FINE, FINE)
            decode_r[pl.ds(at, FINE), :] = (ar * fine_real - ai * fine_imag).astype(jnp.bfloat16)
            decode_i[pl.ds(at, FINE), :] = (ar * fine_imag + ai * fine_real).astype(jnp.bfloat16)
            return carry

        lax.fori_loop(0, coarse_n, row, 0)

    def decoded(block, part):
        span = slice(part * width, (part + 1) * width)
        by_real = jnp.dot(block, decode_r[span], preferred_element_type=jnp.float32)
        by_imag = jnp.dot(block, decode_i[span], preferred_element_type=jnp.float32)
        return jnp.concatenate(
            [by_real[:CHUNK] - by_imag[CHUNK:], by_imag[:CHUNK] + by_real[CHUNK:]], axis=0)

    def finish(j):
        strip_copy(j).wait_recv()
        total = half[j] + decoded(strip_in[j], 1)
        mine[j] = total[:, :STRIP]
        for d in range(1, zs):
            slots_out[d - 1, j] = total[:, d * STRIP:(d + 1) * STRIP].astype(jnp.bfloat16)
            slot_copy(d, j).start()

    for j in range(CHUNKS):
        pair_copy(0, j).wait_recv()
        total = own_part[j] + pair_in[0, j].astype(jnp.float32)
        for d in range(1, highs):
            far_copy(d, j).wait_recv()
            total = total + far_in[d - 1, j].astype(jnp.float32)
        strip[j] = (total * column_gain[...]).astype(jnp.bfloat16)
        strip_copy(j).start()
        half[j] = decoded(strip[j], 0)
        if j >= LAG:
            finish(j - LAG)
    for j in range(CHUNKS - LAG, CHUNKS):
        finish(j)

    sums = []
    for j in range(CHUNKS):
        total = mine[j]
        for d in range(1, zs):
            slot_copy(d, j).wait_recv()
            total = total + slots_in[d - 1, j].astype(jnp.float32)
        sums.append(total)
    for part in range(2):
        value = jnp.concatenate([s[part * CHUNK:(part + 1) * CHUNK] for s in sums], axis=0)
        out[part] = value.T

    for j in range(CHUNKS):
        for d in range(highs):
            pair_copy(d, j).wait_send()
        for d in range(1, highs):
            far_copy(d, j).wait_send()
        strip_copy(j).wait_send()
        for d in range(1, zs):
            slot_copy(d, j).wait_send()


def place_kernel(place, part, out):
    blank = jnp.zeros((SUBGRID - STRIP, STRIP), jnp.float32)
    for n in range(2):
        out[n] = pltpu.roll(jnp.concatenate([part[n], blank], axis=0), place[0], 0)


def solution(mesh):
    cols, facs = mesh.shape["col"], mesh.shape["fac"]
    highs, zs = cols // 2, facs // 2

    def on_device(facets, row_taper, column_taper, column_place, row_offset, column_offset, slot_subgrid):
        rows, width = facets.shape[1], facets.shape[2]
        bf16, f32 = jnp.bfloat16, jnp.float32
        lanes = zs * STRIP
        part = (CHUNKS, 2 * CHUNK, width)
        slot = (CHUNKS, 2 * CHUNK, STRIP)
        far = max(highs - 1, 1)
        sem = pltpu.SemaphoreType.DMA
        grid = pl.pallas_call(
            functools.partial(kernel, cols, facs),
            out_shape=jax.ShapeDtypeStruct((2, STRIP, STRIP), f32),
            in_specs=[pl.BlockSpec(memory_space=pltpu.HBM)] * 6,
            out_specs=pl.BlockSpec(memory_space=pltpu.VMEM),
            scratch_shapes=[
                pltpu.SMEM(row_offset.shape, jnp.int32), pltpu.SMEM(column_offset.shape, jnp.int32),
                pltpu.SMEM(slot_subgrid.shape, jnp.int32),
                pltpu.VMEM((1, rows), f32), pltpu.VMEM((1, width), f32),
                pltpu.VMEM((2, rows, width), bf16),
                pltpu.VMEM((STRIP // FINE, rows), f32), pltpu.VMEM((STRIP // FINE, rows), f32),
                pltpu.VMEM((FINE, rows), f32), pltpu.VMEM((FINE, rows), f32),
                pltpu.VMEM((width // FINE, lanes), f32), pltpu.VMEM((width // FINE, lanes), f32),
                pltpu.VMEM((cols, 2 * STRIP, rows), bf16),
                pltpu.VMEM((2 * width, lanes), bf16), pltpu.VMEM((2 * width, lanes), bf16),
                pltpu.VMEM((highs, *part), bf16), pltpu.VMEM((highs, *part), bf16),
                pltpu.VMEM((far, *part), f32),
                pltpu.VMEM((far, *part), bf16), pltpu.VMEM((far, *part), bf16),
                pltpu.VMEM(part, f32),
                pltpu.VMEM(part, bf16), pltpu.VMEM(part, bf16),
                pltpu.VMEM((CHUNKS, 2 * CHUNK, lanes), f32),
                pltpu.VMEM(slot, f32),
                pltpu.VMEM((zs - 1, *slot), bf16), pltpu.VMEM((zs - 1, *slot), bf16),
                sem((5,)), sem((2,)),
                sem((highs, CHUNKS)), sem((highs, CHUNKS)),
                sem((far, CHUNKS)), sem((far, CHUNKS)),
                sem((CHUNKS,)), sem((CHUNKS,)),
                sem((zs - 1, CHUNKS)), sem((zs - 1, CHUNKS)),
            ],
            compiler_params=pltpu.CompilerParams(
                collective_id=0, has_side_effects=True, vmem_limit_bytes=67_043_328),
        )(row_offset, column_offset, slot_subgrid,
          row_taper.reshape(1, -1), column_taper.reshape(1, -1), facets)
        grid = pl.pallas_call(
            place_kernel,
            out_shape=jax.ShapeDtypeStruct((2, SUBGRID, STRIP), f32),
            in_specs=[pl.BlockSpec(memory_space=pltpu.SMEM), pl.BlockSpec(memory_space=pltpu.VMEM)],
            out_specs=pl.BlockSpec(memory_space=pltpu.VMEM),
        )(column_place, grid)
        return grid.reshape(1, 1, 2, SUBGRID, STRIP)

    in_specs = (P(None, "col", "fac"), P("col"), P(), P(), P(), P(), P())
    out_specs = P("col", "fac", None, None, None)
    return jax.shard_map(on_device, mesh=mesh, in_specs=in_specs, out_specs=out_specs, check_vma=False)
```
